32 devices in a mesh: row: 2 (over y), col: 16 (over z, x, core).
Axes of the slice: x: 2, y: 2, z: 4, core: 2. Of those that a mesh axis runs over, the one named last changes fastest.
Arguments:
- blocks: float32 [512, 128, 128], P(('row', 'col')), may hold values from -0.3125 to 0.3125
- block_row: int32 [512], P(('row', 'col')), may hold values from 0 to 63, as said below
- block_col: int32 [512], P(('row', 'col')), may hold values from 0 to 63, as said below
- counts: int32 [32], P(('row', 'col')), may hold values from 1 to 16, as said below
- diagonal: float32 [8192], P(('row', 'col')), may hold values from 0.25 to 4
- vector: float32 [8192, 256], P(('row', 'col')), may hold values from -8 to 8
Outputs:
- next_basis: float32 [8192, 256], P(('row', 'col'))
- second_image: float32 [8192, 256], P(('row', 'col'))
- arnoldi_column: float32 [2, 256], replicated
The draws below stay inside these ranges and needn't reach their ends.
Inputs may be any that keep to these rules, and one draw needn't show every extreme that they name: The slots of device d = r * 16 + c are rows d * 16 to (d + 1) * 16 - 1. Its slot d * 16 + k * 16 + o (k below 1) has block_row // 2 equal to r * 16 + o, and (block_col // 2) % 16 equals c. No pair (block_row, block_col) occurs twice among all slots. `block_col`: paired with block_row as stated there. Only the first counts[d] slots of device d hold blocks; later slots are ignored. Some device has exactly 16.
All inputs are finite; a program needn't handle non-finite values.
Results may differ from the reference program's by a relative error of at most 0.0001.
Values sent between devices are 32-bit elements; how exact they have to be, the bound alone decides.
A program may use at most 64 MiB of HBM per device.

```python
import math
import jax
import jax.numpy as jnp
from jax import lax

BLK = 128
VB = 2
CAP = 1
RHS = 256
MAXB = 16
NV = 8192
N_ROW = 2
N_COL = 16


def positions_of(key):
    device_count = N_ROW * N_COL
    choices_each = VB * N_ROW * VB
    keys = jax.random.split(jax.random.fold_in(key, 11), device_count * N_COL)

    def one_list(single):
        return jax.random.permutation(single, choices_each).astype(jnp.int32)[:CAP]
    spots = jax.vmap(one_list)(keys).astype(jnp.int32).reshape(device_count, N_COL, CAP)
    spots = jnp.transpose(spots, (0, 2, 1)).reshape(device_count, CAP * N_COL)
    device_ids = jnp.arange(device_count, dtype=jnp.int32)[:, None]
    grid_row = device_ids // N_COL
    grid_col = device_ids % N_COL
    target_col = (jnp.arange(CAP * N_COL, dtype=jnp.int32) % N_COL)[None, :]
    local_row = spots // (N_ROW * VB)
    local_col = spots % (N_ROW * VB)
    global_row = (grid_row * N_COL + target_col) * VB + local_row
    global_col = (local_col // VB * N_COL + grid_col) * VB + local_col % VB
    return (global_row.reshape(-1).astype(jnp.int32), global_col.reshape(-1).astype(jnp.int32))


def draw_block_row(key, part):
    return positions_of(key)[0]


def draw_block_col(key, part):
    return positions_of(key)[1]


def draw_counts(key, part):
    device_count = N_ROW * N_COL
    first_key, second_key, third_key = jax.random.split(jax.random.fold_in(key, 5), 3)
    exponent = jax.random.randint(first_key, (device_count,), 0, 4)
    base_count = MAXB // jnp.left_shift(jnp.ones((device_count,), jnp.int32), exponent)
    reduction = jax.random.randint(second_key, (device_count,), 0, base_count // 2 + 1)
    chosen = jnp.maximum(base_count - reduction, 1)
    busiest = jax.random.randint(third_key, (), 0, device_count)
    return jnp.where(jnp.arange(device_count) == busiest, MAXB, chosen).astype(jnp.int32)


def draw_vector(key, part):
    first_key = jax.random.fold_in(jax.random.fold_in(key, 3), 0)
    ramp = 0.6 + 1.2 * jnp.arange(NV, dtype=jnp.float32)[:, None] / NV
    values = jnp.clip(jax.random.normal(first_key, (NV, RHS), jnp.float32), -4.0, 4.0)
    return (values * ramp).astype(jnp.float32)


def steps_of(own_key, dims, pieces, low, high):
    loudness, own = 1.0, jax.random.fold_in(own_key, 6)
    for axis_at, blocks in pieces:
        draws = jnp.exp(jax.random.uniform(jax.random.fold_in(own, axis_at), (blocks,), jnp.float32, low / len(pieces), high / len(pieces)))
        loudness = loudness * jnp.repeat(draws, dims[axis_at] // blocks).reshape([-1 if axis == axis_at else 1 for axis in range(len(dims))])
    return loudness


def noise(rng, extent, width, bound, pieces=(), kind=jnp.bfloat16):
    array = width * jax.random.normal(rng, extent, jnp.float32)
    if pieces:
        array = array * steps_of(rng, extent, pieces, -0.22, 0.18)
    return jnp.clip(array, -bound, bound).astype(kind)


def setup_inputs(seed: int = 0) -> dict:
    streams_of = jax.random.split(jax.random.key(seed), 7)
    blocks = noise(streams_of[0], (N_ROW * N_COL * MAXB, BLK, BLK), (BLK * MAXB // (3 * VB)) ** -0.5, 0.3125, ((0, 32),), jnp.float32)
    block_row = draw_block_row(jax.random.fold_in(streams_of[6], 71), 0)
    block_col = draw_block_col(jax.random.fold_in(streams_of[6], 71), 0)
    counts = draw_counts(jax.random.fold_in(streams_of[6], 71), 0)
    diagonal = jnp.clip(jnp.exp(math.log(4.0) - 2.7725887 * jax.random.uniform(streams_of[4], (NV,), jnp.float32) ** steps_of(streams_of[4], (NV,), ((0, 32),), -0.2, 0.2)), 0.25, 4.0)
    vector = draw_vector(jax.random.fold_in(streams_of[6], 71), 0)
    return dict(blocks=blocks, block_row=block_row, block_col=block_col, counts=counts, diagonal=diagonal, vector=vector)


def apply_transpose(source, diagonal, blocks, block_row, block_col, counts):
    device_count = counts.shape[0]
    tile_size = blocks.shape[1]
    slot_count = blocks.shape[0] // device_count
    rhs_count = source.shape[1]
    block_total = source.shape[0] // tile_size
    stacked = source.reshape(block_total, tile_size, rhs_count)
    live_slot = (jnp.arange(slot_count, dtype=jnp.int32)[None, :] < counts[:, None]).astype(jnp.float32)

    def advance(totals, inputs):
        tile_set, row_ids, col_ids, weights = inputs
        picked = stacked[row_ids]
        products = jnp.einsum('mab,mak->mbk', tile_set, picked, precision=lax.Precision.HIGHEST)
        products = products * weights[:, None, None]
        return (totals.at[col_ids].add(products), None)
    start_sum = jnp.zeros((block_total, tile_size, rhs_count), jnp.float32)
    totals, _ = lax.scan(advance, start_sum, (blocks.reshape(device_count, slot_count, tile_size, tile_size), block_row.reshape(device_count, slot_count), block_col.reshape(device_count, slot_count), live_slot))
    return diagonal[:, None] * source + totals.reshape(source.shape)

def reference(blocks, block_row, block_col, counts, diagonal, vector):
    magnitude = jnp.sqrt(lax.optimization_barrier(jnp.mean(vector * vector, axis=0)) + 1e-06)
    unit_basis = vector / magnitude
    first_image = apply_transpose(unit_basis, diagonal, blocks, block_row, block_col, counts)
    projection = lax.optimization_barrier(jnp.mean(first_image * unit_basis, axis=0))
    remainder = first_image - projection * unit_basis
    norm_new = jnp.sqrt(lax.optimization_barrier(jnp.mean(remainder * remainder, axis=0)) + 1e-06)
    next_basis = remainder / norm_new
    second_image = apply_transpose(next_basis, diagonal, blocks, block_row, block_col, counts)
    return (next_basis, second_image, jnp.stack([projection, norm_new]))
```

```python
import functools

import jax
import jax.numpy as jnp
from jax import lax
from jax.experimental import pallas as pl
from jax.experimental.pallas import tpu as pltpu
from jax.sharding import PartitionSpec as P

MESH = pl.DeviceIdType.MESH
LANES = 128
STAT_ROWS = 8


def chip_grid(chips):
    x = max(d for d in range(1, chips + 1) if chips % d == 0 and d * d <= chips)
    return chips // x, x


def nearest(turn, here, size):
    both = jnp.minimum(here, size - 1 - here)
    reach = (turn + 1) // 2
    near = jnp.where(turn % 2 == 1, here + reach, here - reach)
    far = jnp.where(here < size - 1 - here, turn, size - 1 - turn)
    return jnp.where(turn <= 2 * both, near, far)


def split(value):
    high = value.astype(jnp.bfloat16)
    low = (value - high.astype(jnp.float32)).astype(jnp.bfloat16)
    return high, low


def kernel(
    n_rows, n_cols, total_rows,
    brow, bcol, counts, blocks_hbm, diag_ref, vec_hbm,
    next_ref, second_ref, column_ref,
    blocks, held, w_high, w_low, totals, partner, diag, stat_col, stat_row,
    local_sem, unit_send, unit_recv, y_send, y_recv, col_send, col_recv, row_send, row_recv,
):
    tile = blocks.shape[1]
    slots = blocks.shape[0]
    cap = slots // n_cols
    per = held.shape[3]
    halves = held.shape[1]
    n_local = n_rows * per
    chips = n_cols // 2
    size_z, size_x = chip_grid(chips)
    row, col = lax.axis_index("row"), lax.axis_index("col")
    core, chip = col % 2, col // 2
    at_x, at_z = chip % size_x, chip // size_x

    own = []
    for h in range(halves):
        for b in range(per):
            own.append(pltpu.make_async_copy(
                vec_hbm.at[pl.ds(b * tile, tile), pl.ds(h * LANES, LANES)],
                held.at[0, h, col, b], local_sem.at[h * per + b]))
    own.append(pltpu.make_async_copy(blocks_hbm, blocks, local_sem.at[halves * per]))
    for copy in own:
        copy.start()

    barrier = pltpu.get_barrier_semaphore()

    @pl.loop(1, n_cols)
    def _(step):
        pl.semaphore_signal(barrier, inc=1, device_id=(row, (col + step) % n_cols), device_id_type=MESH)

    @pl.loop(1, n_rows)
    def _(step):
        pl.semaphore_signal(barrier, inc=1, device_id=((row + step) % n_rows, col), device_id_type=MESH)

    pl.semaphore_wait(barrier, n_cols + n_rows - 2)

    def branches(g, h, sx, sz, act):
        source_chip = sz * size_x + sx
        source = source_chip * 2 + core
        if halves > 1 and h == halves - 1:
            x_first = (sz == 0) | (sz == size_z - 1)
        else:
            x_first = sz < 0
        along_z = x_first | (at_x == sx)
        along_x = jnp.logical_not(x_first) | (at_z == sz)
        targets = (
            (along_z & (at_z >= sz) & (at_z + 1 < size_z), at_x, at_z + 1, core),
            (along_z & (at_z <= sz) & (at_z >= 1), at_x, at_z - 1, core),
            (along_x & (at_x >= sx) & (at_x + 1 < size_x), at_x + 1, at_z, core),
            (along_x & (at_x <= sx) & (at_x >= 1), at_x - 1, at_z, core),
            (None, at_x, at_z, 1 - core),
        )
        piece = held.at[g, h, source]
        for i, (wanted, tx, tz, tcore) in enumerate(targets):
            def go(i=i, tx=tx, tz=tz, tcore=tcore):
                act(pltpu.make_async_remote_copy(
                    piece, piece, unit_send.at[g, h, source_chip, i], unit_recv.at[g, h, source],
                    device_id=(row, (tz * size_x + tx) * 2 + tcore), device_id_type=MESH))
            if wanted is None:
                go()
            else:
                pl.when(wanted)(go)

    def start(copy):
        copy.start()

    def drain(copy):
        copy.wait_send()

    def arrived(g, h, source):
        piece = held.at[g, h, source]
        pltpu.make_async_remote_copy(
            piece, piece, unit_send.at[g, h, 0, 0], unit_recv.at[g, h, source],
            device_id=(row, col), device_id_type=MESH).wait_recv()

    def send_own(g, h):
        branches(g, h, at_x, at_z, start)

    def multiply(g, h, p):
        parts = []
        for q in range(cap):
            for kk in range(2):
                o = p * 2 + kk
                which = brow[q * n_cols + o] % per
                part = held[g, h, o, 0]
                for b in range(1, per):
                    part = jnp.where(which == b, held[g, h, o, b], part)
                parts.append(part)
        high, low = split(jnp.concatenate(parts, axis=0))
        dot = functools.partial(jnp.dot, preferred_element_type=jnp.float32)
        product = dot(w_high[p], high) + dot(w_high[p], low) + dot(w_low[p], high)
        return product.reshape(n_rows, per, tile, LANES)

    def first_turn(g, h):
        arrived(g, h, chip * 2 + 1 - core)
        totals[h] = multiply(g, h, chip)

    def turns(g, h, low, high):
        @pl.loop(low, high)
        def _(turn):
            sz = nearest(turn // size_x, at_z, size_z)
            sx = nearest(turn % size_x, at_x, size_x)
            p = sz * size_x + sx
            arrived(g, h, p * 2 + core)
            branches(g, h, sx, sz, start)
            arrived(g, h, p * 2 + 1 - core)
            totals[h] += multiply(g, h, p)

    def y_copy(g, h, step):
        target = (row + step) % n_rows
        return pltpu.make_async_remote_copy(
            totals.at[h, target], partner.at[g, h, row], y_send.at[g, h, step - 1], y_recv.at[g, h, step - 1],
            device_id=(target, col), device_id_type=MESH)

    def y_start(g, h):
        for step in range(1, n_rows):
            y_copy(g, h, step).start()

    def y_drain(g, h):
        for step in range(1, n_rows):
            y_copy(g, h, step).wait_send()

    def y_sum(g, h):
        total = totals[h, row]
        for step in range(1, n_rows):
            origin = (row + n_rows - step) % n_rows
            pltpu.make_async_remote_copy(
                totals.at[h, row], partner.at[g, h, origin], y_send.at[g, h, step - 1], y_recv.at[g, h, step - 1],
                device_id=(row, col), device_id_type=MESH).wait_recv()
            total = total + partner[g, h, origin]
        return total

    def stats_begin(i, rows):
        filler = jnp.zeros((STAT_ROWS - len(rows), LANES), jnp.float32)
        stat_col[i, col] = jnp.concatenate(list(rows) + [filler], axis=0)

        @pl.loop(1, n_cols)
        def _(step):
            pltpu.make_async_remote_copy(
                stat_col.at[i, col], stat_col.at[i, col], col_send.at[i], col_recv.at[i],
                device_id=(row, (col + step) % n_cols), device_id_type=MESH).start()

    def stats_turn(i):
        many = stat_col.at[i, pl.ds(0, n_cols - 1)]
        pltpu.make_async_copy(many, many, col_recv.at[i]).wait()
        stat_row[i, row] = jnp.sum(stat_col[i], axis=0)

        @pl.loop(1, n_rows)
        def _(step):
            pltpu.make_async_remote_copy(
                stat_row.at[i, row], stat_row.at[i, row], row_send.at[i], row_recv.at[i],
                device_id=((row + step) % n_rows, col), device_id_type=MESH).start()

    def stats_end(i):
        many = stat_row.at[i, pl.ds(0, n_rows - 1)]
        pltpu.make_async_copy(many, many, row_recv.at[i]).wait()
        return jnp.sum(stat_row[i], axis=0)

    def stats_drain(i):
        many = stat_col.at[i, pl.ds(0, n_cols - 1)]
        pltpu.make_async_copy(many, many, col_send.at[i]).wait()
        many = stat_row.at[i, pl.ds(0, n_rows - 1)]
        pltpu.make_async_copy(many, many, row_send.at[i]).wait()

    def over_rows(value):
        return jnp.sum(value.reshape(per * tile, LANES), axis=0, keepdims=True)

    for copy in own[:-1]:
        copy.wait()
    send_own(0, 0)
    squares = []
    for h in range(halves):
        mine = held[0, h, col]
        squares.append(over_rows(mine * mine))
    stats_begin(0, squares)
    for b in range(per):
        diag[b] = jnp.broadcast_to(diag_ref[pl.ds(b, 1), :], (tile, LANES)).T
    own[-1].wait()

    @pl.loop(0, chips)
    def _(p):
        for q in range(cap):
            for kk in range(2):
                local = p * 2 + kk
                slot = q * n_cols + local
                piece = bcol[slot] // per
                target = piece // n_cols * per + bcol[slot] % per
                target = jnp.where(slot < counts[0], target, -1)
                high, low = split(blocks[slot].T)
                at = pl.ds((q * 2 + kk) * tile, tile)
                for j in range(n_local):
                    keep = jnp.where(target == j, 1.0, 0.0).astype(jnp.bfloat16)
                    w_high[p, pl.ds(j * tile, tile), at] = high * keep
                    w_low[p, pl.ds(j * tile, tile), at] = low * keep

    middle = max(1, chips // 2)
    magnitude, image_rows = [], []
    for g in range(2):
        for h in range(halves):
            if g == 1:
                y_drain(0, h)
            first_turn(g, h)
            turns(g, h, 1, middle)
            last = (g, h - 1) if h else (g - 1, halves - 1)
            if (g, h) == (0, 0):
                stats_turn(0)
            elif last[0] == 0:
                lh = last[1]
                if not magnitude:
                    total_squares = stats_end(0)
                    magnitude = [jnp.sqrt(total_squares[k:k + 1] / total_rows + 1e-06) for k in range(halves)]
                mine = held[0, lh, col]
                image = (diag[...] * mine + y_sum(0, lh)) / magnitude[lh]
                held[1, lh, col] = image
                send_own(1, lh)
                image_rows.append(over_rows(image * image))
                image_rows.append(over_rows(image * (mine / magnitude[lh])))
                if len(image_rows) == 2 * halves:
                    stats_begin(1, image_rows)
            else:
                if h == 1:
                    stats = stats_end(1)
                    projection, norm_new = [], []
                    for k in range(halves):
                        image_squares, cross = stats[2 * k:2 * k + 1], stats[2 * k + 1:2 * k + 2]
                        basis_squares = total_squares[k:k + 1] / (magnitude[k] * magnitude[k])
                        part = cross / total_rows
                        power = (image_squares - 2.0 * part * cross + part * part * basis_squares) / total_rows
                        projection.append(part)
                        norm_new.append(jnp.sqrt(jnp.maximum(power, 0.0) + 1e-06))
                        at = pl.ds(k * LANES, LANES)
                        image = held[1, k, col].reshape(per * tile, LANES)
                        basis = held[0, k, col].reshape(per * tile, LANES) / magnitude[k]
                        next_ref[:, at] = (image - part * basis) / norm_new[k]
                        column_ref[pl.ds(0, 1), at] = part
                        column_ref[pl.ds(1, 1), at] = norm_new[k]
                finish(g, last[1], held, diag, projection, norm_new, y_sum, second_ref, col)
            if g == 0 and h + 1 < halves:
                send_own(0, h + 1)
            turns(g, h, middle, chips)
            y_start(g, h)
            if (g, h) == (1, 0):
                stats_turn(1)
    finish(1, halves - 1, held, diag, projection, norm_new, y_sum, second_ref, col)

    for g in range(2):
        stats_drain(g)
        for h in range(halves):
            if g == 1:
                y_drain(g, h)

            @pl.loop(0, chips)
            def _(p):
                branches(g, h, p % size_x, p // size_x, drain)


def finish(g, h, held, diag, projection, norm_new, y_sum, second_ref, col):
    image = held[g, h, col]
    result = (diag[...] * image + y_sum(g, h) - projection[h] * image) / norm_new[h]
    second_ref[:, pl.ds(h * LANES, LANES)] = result.reshape(second_ref.shape[0], LANES)


def per_device(blocks, block_row, block_col, counts, diagonal, vector):
    n_rows, n_cols = lax.axis_size("row"), lax.axis_size("col")
    slots, tile, _ = blocks.shape
    mine, rhs = vector.shape
    per, halves = mine // tile, rhs // LANES
    cap, chips, n_local = slots // n_cols, n_cols // 2, n_rows * per
    smem = pl.BlockSpec(memory_space=pltpu.SMEM)
    vmem = pl.BlockSpec(memory_space=pltpu.VMEM)
    anywhere = pl.BlockSpec(memory_space=pl.ANY)
    f32, dma = jnp.float32, pltpu.SemaphoreType.DMA
    weight = pltpu.VMEM((chips, n_local * tile, 2 * cap * tile), jnp.bfloat16)
    return pl.pallas_call(
        functools.partial(kernel, n_rows, n_cols, mine * n_rows * n_cols),
        out_shape=(
            jax.ShapeDtypeStruct((mine, rhs), f32),
            jax.ShapeDtypeStruct((mine, rhs), f32),
            jax.ShapeDtypeStruct((2, rhs), f32),
        ),
        in_specs=[smem, smem, smem, anywhere, vmem, anywhere],
        out_specs=(vmem, vmem, vmem),
        scratch_shapes=[
            pltpu.VMEM((slots, tile, tile), f32),
            pltpu.VMEM((2, halves, n_cols, per, tile, LANES), f32),
            weight,
            weight,
            pltpu.VMEM((halves, n_rows, per, tile, LANES), f32),
            pltpu.VMEM((2, halves, n_rows, per, tile, LANES), f32),
            pltpu.VMEM((per, tile, LANES), f32),
            pltpu.VMEM((2, n_cols, STAT_ROWS, LANES), f32),
            pltpu.VMEM((2, n_rows, STAT_ROWS, LANES), f32),
            dma((halves * per + 1,)),
            dma((2, halves, chips, 5)),
            dma((2, halves, n_cols)),
            dma((2, halves, n_rows)),
            dma((2, halves, n_rows)),
            dma((2,)), dma((2,)), dma((2,)), dma((2,)),
        ],
        compiler_params=pltpu.CompilerParams(
            collective_id=0, has_side_effects=True, vmem_limit_bytes=60 * 1024 * 1024),
    )(block_row, block_col, counts, blocks, diagonal.reshape(per, tile), vector)


def solution(mesh):
    spec = P(("row", "col"))
    return jax.shard_map(
        per_device,
        mesh=mesh,
        in_specs=(P(("row", "col"), None, None), spec, spec, spec, spec, P(("row", "col"), None)),
        out_specs=(P(("row", "col"), None), P(("row", "col"), None), P()),
        check_vma=False,
    )
```

```python
import functools

import jax
import jax.numpy as jnp
from jax import lax
from jax.experimental import pallas as pl
from jax.experimental.pallas import tpu as pltpu
from jax.sharding import PartitionSpec as P

MESH = pl.DeviceIdType.MESH
LANES = 128
CUTS = 1
STAT_ROWS = 8


def chip_grid(chips):
    x = max(d for d in range(1, chips + 1) if chips % d == 0 and d * d <= chips)
    return chips // x, x


def nearest(turn, here, size):
    both = jnp.minimum(here, size - 1 - here)
    reach = (turn + 1) // 2
    near = jnp.where(turn % 2 == 1, here + reach, here - reach)
    far = jnp.where(here < size - 1 - here, turn, size - 1 - turn)
    return jnp.where(turn <= 2 * both, near, far)


def split(value):
    high = value.astype(jnp.bfloat16)
    low = (value - high.astype(jnp.float32)).astype(jnp.bfloat16)
    return high, low


def kernel(
    n_rows, n_cols, total_rows,
    brow, bcol, counts, blocks_hbm, diag_ref, vec_hbm,
    next_ref, second_ref, column_ref,
    blocks, held, w_high, w_low, totals, partner, diag, stat_col, stat_row,
    local_sem, unit_send, unit_recv, pair_send, pair_recv, y_send, y_recv, col_send, col_recv, row_send, row_recv,
):
    tile = blocks.shape[1]
    slots = blocks.shape[0]
    cap = slots // n_cols
    per = held.shape[3]
    halves = held.shape[1]
    n_local = n_rows * per
    chips = n_cols // 2
    size_z, size_x = chip_grid(chips)
    row, col = lax.axis_index("row"), lax.axis_index("col")
    core, chip = col % 2, col // 2
    at_x, at_z = chip % size_x, chip // size_x

    own = []
    for h in range(halves):
        for b in range(per):
            own.append(pltpu.make_async_copy(
                vec_hbm.at[pl.ds(b * tile, tile), pl.ds(h * LANES, LANES)],
                held.at[0, h, col, b], local_sem.at[h * per + b]))
    own.append(pltpu.make_async_copy(blocks_hbm, blocks, local_sem.at[halves * per]))
    for copy in own:
        copy.start()

    barrier = pltpu.get_barrier_semaphore()

    @pl.loop(1, n_cols)
    def _(step):
        pl.semaphore_signal(barrier, inc=1, device_id=(row, (col + step) % n_cols), device_id_type=MESH)

    @pl.loop(1, n_rows)
    def _(step):
        pl.semaphore_signal(barrier, inc=1, device_id=((row + step) % n_rows, col), device_id_type=MESH)

    pl.semaphore_wait(barrier, n_cols + n_rows - 2)

    def cut(g, h, source, part):
        return held.at[g, h, source, part // CUTS, pl.ds(part % CUTS * (tile // CUTS), tile // CUTS)]

    def branches(g, h, sx, sz, act, part):
        source_chip = sz * size_x + sx
        source = source_chip * 2 + core
        if halves > 1 and h == halves - 1:
            x_first = (sz == 0) | (sz == size_z - 1)
        else:
            x_first = sz < 0
        along_z = x_first | (at_x == sx)
        along_x = jnp.logical_not(x_first) | (at_z == sz)
        targets = (
            (along_z & (at_z >= sz) & (at_z + 1 < size_z), at_x, at_z + 1, core),
            (along_z & (at_z <= sz) & (at_z >= 1), at_x, at_z - 1, core),
            (along_x & (at_x >= sx) & (at_x + 1 < size_x), at_x + 1, at_z, core),
            (along_x & (at_x <= sx) & (at_x >= 1), at_x - 1, at_z, core),
        )
        piece = cut(g, h, source, part)
        for i, (wanted, tx, tz, tcore) in enumerate(targets):
            def go(i=i, tx=tx, tz=tz, tcore=tcore):
                act(pltpu.make_async_remote_copy(
                    piece, piece, unit_send.at[g, h, source_chip, part, i], unit_recv.at[g, h, source, part],
                    device_id=(row, (tz * size_x + tx) * 2 + tcore), device_id_type=MESH))
            pl.when(wanted)(go)

    def share(g, h, source_chip, act):
        source = source_chip * 2 + core
        piece = held.at[g, h, source]
        act(pltpu.make_async_remote_copy(
            piece, piece, pair_send.at[g, h, source_chip], pair_recv.at[g, h, source_chip],
            device_id=(row, chip * 2 + 1 - core), device_id_type=MESH))

    def start(copy):
        copy.start()

    def drain(copy):
        copy.wait_send()

    def arrived(g, h, source, part):
        piece = cut(g, h, source, part)
        pltpu.make_async_remote_copy(
            piece, piece, unit_send.at[g, h, 0, part, 0], unit_recv.at[g, h, source, part],
            device_id=(row, col), device_id_type=MESH).wait_recv()

    def shared(g, h, source_chip):
        piece = held.at[g, h, source_chip * 2 + 1 - core]
        pltpu.make_async_remote_copy(
            piece, piece, pair_send.at[g, h, source_chip], pair_recv.at[g, h, source_chip],
            device_id=(row, col), device_id_type=MESH).wait_recv()

    def send_own(g, h):
        for part in range(per * CUTS):
            branches(g, h, at_x, at_z, start, part)
        share(g, h, chip, start)

    def multiply(g, h, p):
        parts = []
        for q in range(cap):
            for kk in range(2):
                o = p * 2 + kk
                which = brow[q * n_cols + o] % per
                part = held[g, h, o, 0]
                for b in range(1, per):
                    part = jnp.where(which == b, held[g, h, o, b], part)
                parts.append(part)
        high, low = split(jnp.concatenate(parts, axis=0))
        dot = functools.partial(jnp.dot, preferred_element_type=jnp.float32)
        product = dot(w_high[p], high) + dot(w_high[p], low) + dot(w_low[p], high)
        return product.reshape(n_rows, per, tile, LANES)

    def place(turn):
        return nearest(turn // size_x, at_z, size_z), nearest(turn % size_x, at_x, size_x)

    def relay(g, h, turn):
        sz, sx = place(turn)
        p = sz * size_x + sx
        for part in range(per * CUTS):
            arrived(g, h, p * 2 + core, part)
            branches(g, h, sx, sz, start, part)
        share(g, h, p, start)

    def consume(g, h, turn):
        sz, sx = place(turn)
        p = sz * size_x + sx
        shared(g, h, p)
        totals[h] += multiply(g, h, p)

    def turns(low, high, *phases):
        @pl.loop(low, high)
        def _(turn):
            for g, h, shift in phases:
                relay(g, h, turn + shift)
            for g, h, shift in phases:
                consume(g, h, turn + shift - 1)

    def clear(h):
        totals[h] = jnp.zeros_like(totals[h])

    def close(g, h):
        consume(g, h, chips - 1)
        y_start(g, h)

    def y_copy(g, h, step):
        target = (row + step) % n_rows
        return pltpu.make_async_remote_copy(
            totals.at[h, target], partner.at[g, h, row], y_send.at[g, h, step - 1], y_recv.at[g, h, step - 1],
            device_id=(target, col), device_id_type=MESH)

    def y_start(g, h):
        for step in range(1, n_rows):
            y_copy(g, h, step).start()

    def y_drain(g, h):
        for step in range(1, n_rows):
            y_copy(g, h, step).wait_send()

    def y_sum(g, h):
        total = totals[h, row]
        for step in range(1, n_rows):
            origin = (row + n_rows - step) % n_rows
            pltpu.make_async_remote_copy(
                totals.at[h, row], partner.at[g, h, origin], y_send.at[g, h, step - 1], y_recv.at[g, h, step - 1],
                device_id=(row, col), device_id_type=MESH).wait_recv()
            total = total + partner[g, h, origin]
        return total

    def stats_begin(i, rows):
        filler = jnp.zeros((STAT_ROWS - len(rows), LANES), jnp.float32)
        stat_col[i, col] = jnp.concatenate(list(rows) + [filler], axis=0)

        @pl.loop(1, n_cols)
        def _(step):
            pltpu.make_async_remote_copy(
                stat_col.at[i, col], stat_col.at[i, col], col_send.at[i], col_recv.at[i],
                device_id=(row, (col + step) % n_cols), device_id_type=MESH).start()

    def stats_turn(i):
        many = stat_col.at[i, pl.ds(0, n_cols - 1)]
        pltpu.make_async_copy(many, many, col_recv.at[i]).wait()
        stat_row[i, row] = jnp.sum(stat_col[i], axis=0)

        @pl.loop(1, n_rows)
        def _(step):
            pltpu.make_async_remote_copy(
                stat_row.at[i, row], stat_row.at[i, row], row_send.at[i], row_recv.at[i],
                device_id=((row + step) % n_rows, col), device_id_type=MESH).start()

    def stats_end(i):
        many = stat_row.at[i, pl.ds(0, n_rows - 1)]
        pltpu.make_async_copy(many, many, row_recv.at[i]).wait()
        return jnp.sum(stat_row[i], axis=0)

    def stats_drain(i):
        many = stat_col.at[i, pl.ds(0, n_cols - 1)]
        pltpu.make_async_copy(many, many, col_send.at[i]).wait()
        many = stat_row.at[i, pl.ds(0, n_rows - 1)]
        pltpu.make_async_copy(many, many, row_send.at[i]).wait()

    def over_rows(value):
        return jnp.sum(value.reshape(per * tile, LANES), axis=0, keepdims=True)

    for copy in own[:-1]:
        copy.wait()
    send_own(0, 0)
    send_own(0, 1)
    squares = []
    for h in range(halves):
        mine = held[0, h, col]
        squares.append(over_rows(mine * mine))
    stats_begin(0, squares)
    for b in range(per):
        diag[b] = jnp.broadcast_to(diag_ref[pl.ds(b, 1), :], (tile, LANES)).T
    own[-1].wait()

    @pl.loop(0, chips)
    def _(p):
        for q in range(cap):
            for kk in range(2):
                local = p * 2 + kk
                slot = q * n_cols + local
                piece = bcol[slot] // per
                target = piece // n_cols * per + bcol[slot] % per
                target = jnp.where(slot < counts[0], target, -1)
                high, low = split(blocks[slot].T)
                at = pl.ds((q * 2 + kk) * tile, tile)
                for j in range(n_local):
                    keep = jnp.where(target == j, 1.0, 0.0).astype(jnp.bfloat16)
                    w_high[p, pl.ds(j * tile, tile), at] = high * keep
                    w_low[p, pl.ds(j * tile, tile), at] = low * keep

    half = chips // 2
    rest = min(chips, chips - half + 1)
    late = max(rest, chips - 1)
    clear(0)
    clear(1)
    turns(1, half, (0, 0, 0))
    turns(half, chips, (0, 0, 0), (0, 1, 1 - half))
    close(0, 0)
    stats_turn(0)
    turns(rest, late, (0, 1, 0))
    total_squares = stats_end(0)
    magnitude = [jnp.sqrt(total_squares[k:k + 1] / total_rows + 1e-06) for k in range(2)]
    image_rows = []

    def make_image(h):
        mine = held[0, h, col]
        image = (diag[...] * mine + y_sum(0, h)) / magnitude[h]
        held[1, h, col] = image
        send_own(1, h)
        image_rows.append(over_rows(image * image))
        image_rows.append(over_rows(image * (mine / magnitude[h])))

    make_image(0)
    y_drain(0, 0)
    clear(0)
    turns(late, chips, (0, 1, 0))
    close(0, 1)
    early = min(3, half)
    turns(1, early, (1, 0, 0))
    make_image(1)
    stats_begin(1, image_rows)
    y_drain(0, 1)
    clear(1)
    turns(early, half, (1, 0, 0))
    turns(half, chips, (1, 0, 0), (1, 1, 1 - half))
    close(1, 0)
    stats_turn(1)
    turns(rest, late, (1, 1, 0))
    stats = stats_end(1)
    projection, norm_new = [], []
    for k in range(2):
        image_squares, cross = stats[2 * k:2 * k + 1], stats[2 * k + 1:2 * k + 2]
        basis_squares = total_squares[k:k + 1] / (magnitude[k] * magnitude[k])
        part = cross / total_rows
        power = (image_squares - 2.0 * part * cross + part * part * basis_squares) / total_rows
        projection.append(part)
        norm_new.append(jnp.sqrt(jnp.maximum(power, 0.0) + 1e-06))
        at = pl.ds(k * LANES, LANES)
        image = held[1, k, col].reshape(per * tile, LANES)
        basis = held[0, k, col].reshape(per * tile, LANES) / magnitude[k]
        next_ref[:, at] = (image - part * basis) / norm_new[k]
        column_ref[pl.ds(0, 1), at] = part
        column_ref[pl.ds(1, 1), at] = norm_new[k]
    finish(1, 0, held, diag, projection, norm_new, y_sum, second_ref, col)
    turns(late, chips, (1, 1, 0))
    close(1, 1)
    finish(1, 1, held, diag, projection, norm_new, y_sum, second_ref, col)

    for g in range(2):
        stats_drain(g)
        for h in range(2):
            if g == 1:
                y_drain(g, h)

            @pl.loop(0, chips)
            def _(p):
                for part in range(per * CUTS):
                    branches(g, h, p % size_x, p // size_x, drain, part)
                share(g, h, p, drain)


def finish(g, h, held, diag, projection, norm_new, y_sum, second_ref, col):
    image = held[g, h, col]
    result = (diag[...] * image + y_sum(g, h) - projection[h] * image) / norm_new[h]
    second_ref[:, pl.ds(h * LANES, LANES)] = result.reshape(second_ref.shape[0], LANES)


def per_device(blocks, block_row, block_col, counts, diagonal, vector):
    n_rows, n_cols = lax.axis_size("row"), lax.axis_size("col")
    slots, tile, _ = blocks.shape
    mine, rhs = vector.shape
    per, halves = mine // tile, rhs // LANES
    cap, chips, n_local = slots // n_cols, n_cols // 2, n_rows * per
    smem = pl.BlockSpec(memory_space=pltpu.SMEM)
    vmem = pl.BlockSpec(memory_space=pltpu.VMEM)
    anywhere = pl.BlockSpec(memory_space=pl.ANY)
    f32, dma = jnp.float32, pltpu.SemaphoreType.DMA
    weight = pltpu.VMEM((chips, n_local * tile, 2 * cap * tile), jnp.bfloat16)
    return pl.pallas_call(
        functools.partial(kernel, n_rows, n_cols, mine * n_rows * n_cols),
        out_shape=(
            jax.ShapeDtypeStruct((mine, rhs), f32),
            jax.ShapeDtypeStruct((mine, rhs), f32),
            jax.ShapeDtypeStruct((2, rhs), f32),
        ),
        in_specs=[smem, smem, smem, anywhere, vmem, anywhere],
        out_specs=(vmem, vmem, vmem),
        scratch_shapes=[
            pltpu.VMEM((slots, tile, tile), f32),
            pltpu.VMEM((2, halves, n_cols, per, tile, LANES), f32),
            weight,
            weight,
            pltpu.VMEM((halves, n_rows, per, tile, LANES), f32),
            pltpu.VMEM((2, halves, n_rows, per, tile, LANES), f32),
            pltpu.VMEM((per, tile, LANES), f32),
            pltpu.VMEM((2, n_cols, STAT_ROWS, LANES), f32),
            pltpu.VMEM((2, n_rows, STAT_ROWS, LANES), f32),
            dma((halves * per + 1,)),
            dma((2, halves, chips, per * CUTS, 4)),
            dma((2, halves, n_cols, per * CUTS)),
            dma((2, halves, chips)),
            dma((2, halves, chips)),
            dma((2, halves, n_rows)),
            dma((2, halves, n_rows)),
            dma((2,)), dma((2,)), dma((2,)), dma((2,)),
        ],
        compiler_params=pltpu.CompilerParams(
            collective_id=0, has_side_effects=True, vmem_limit_bytes=60 * 1024 * 1024),
    )(block_row, block_col, counts, blocks, diagonal.reshape(per, tile), vector)


def solution(mesh):
    spec = P(("row", "col"))
    return jax.shard_map(
        per_device,
        mesh=mesh,
        in_specs=(P(("row", "col"), None, None), spec, spec, spec, spec, P(("row", "col"), None)),
        out_specs=(P(("row", "col"), None), P(("row", "col"), None), P()),
        check_vma=False,
    )
```

```python
import functools

import jax
import jax.numpy as jnp
from jax import lax
from jax.experimental import pallas as pl
from jax.experimental.pallas import tpu as pltpu
from jax.sharding import PartitionSpec as P

MESH = pl.DeviceIdType.MESH
LANES = 128
CUTS = 1
STAT_ROWS = 8


def chip_grid(chips):
    x = max(d for d in range(1, chips + 1) if chips % d == 0 and d * d <= chips)
    return chips // x, x


def nearest(turn, here, size):
    both = jnp.minimum(here, size - 1 - here)
    reach = (turn + 1) // 2
    near = jnp.where(turn % 2 == 1, here + reach, here - reach)
    far = jnp.where(here < size - 1 - here, turn, size - 1 - turn)
    return jnp.where(turn <= 2 * both, near, far)


def split(value):
    high = value.astype(jnp.bfloat16)
    low = (value - high.astype(jnp.float32)).astype(jnp.bfloat16)
    return high, low


def kernel(
    n_rows, n_cols, total_rows,
    brow, bcol, counts, blocks_hbm, diag_ref, vec_hbm,
    next_ref, second_ref, column_ref,
    blocks, held, w_high, w_low, totals, partner, diag, stat_col, stat_row,
    local_sem, unit_send, unit_recv, pair_send, pair_recv, y_send, y_recv, col_send, col_recv, row_send, row_recv,
):
    tile = blocks.shape[1]
    slots = blocks.shape[0]
    cap = slots // n_cols
    per = held.shape[3]
    halves = held.shape[1]
    n_local = n_rows * per
    chips = n_cols // 2
    size_z, size_x = chip_grid(chips)
    row, col = lax.axis_index("row"), lax.axis_index("col")
    core, chip = col % 2, col // 2
    at_x, at_z = chip % size_x, chip // size_x

    own = []
    for h in range(halves):
        for b in range(per):
            own.append(pltpu.make_async_copy(
                vec_hbm.at[pl.ds(b * tile, tile), pl.ds(h * LANES, LANES)],
                held.at[0, h, col, b], local_sem.at[h * per + b]))
    own.append(pltpu.make_async_copy(blocks_hbm, blocks, local_sem.at[halves * per]))
    for copy in own:
        copy.start()

    barrier = pltpu.get_barrier_semaphore()

    @pl.loop(1, n_cols)
    def _(step):
        pl.semaphore_signal(barrier, inc=1, device_id=(row, (col + step) % n_cols), device_id_type=MESH)

    @pl.loop(1, n_rows)
    def _(step):
        pl.semaphore_signal(barrier, inc=1, device_id=((row + step) % n_rows, col), device_id_type=MESH)

    pl.semaphore_wait(barrier, n_cols + n_rows - 2)

    def cut(g, h, source, part):
        return held.at[g, h, source, part // CUTS, pl.ds(part % CUTS * (tile // CUTS), tile // CUTS)]

    def branches(g, h, sx, sz, act, part):
        source_chip = sz * size_x + sx
        source = source_chip * 2 + core
        if halves > 1 and h == halves - 1:
            x_first = (sz == 0) | (sz == size_z - 1)
        else:
            x_first = sz < 0
        along_z = x_first | (at_x == sx)
        along_x = jnp.logical_not(x_first) | (at_z == sz)
        targets = (
            (along_z & (at_z >= sz) & (at_z + 1 < size_z), at_x, at_z + 1, core),
            (along_z & (at_z <= sz) & (at_z >= 1), at_x, at_z - 1, core),
            (along_x & (at_x >= sx) & (at_x + 1 < size_x), at_x + 1, at_z, core),
            (along_x & (at_x <= sx) & (at_x >= 1), at_x - 1, at_z, core),
        )
        piece = cut(g, h, source, part)
        for i, (wanted, tx, tz, tcore) in enumerate(targets):
            def go(i=i, tx=tx, tz=tz, tcore=tcore):
                act(pltpu.make_async_remote_copy(
                    piece, piece, unit_send.at[g, h, source_chip, part, i], unit_recv.at[g, h, source, part],
                    device_id=(row, (tz * size_x + tx) * 2 + tcore), device_id_type=MESH))
            pl.when(wanted)(go)

    def share(g, h, source_chip, act):
        source = source_chip * 2 + core
        piece = held.at[g, h, source]
        act(pltpu.make_async_remote_copy(
            piece, piece, pair_send.at[g, h, source_chip], pair_recv.at[g, h, source_chip],
            device_id=(row, chip * 2 + 1 - core), device_id_type=MESH))

    def start(copy):
        copy.start()

    def drain(copy):
        copy.wait_send()

    def arrived(g, h, source, part):
        piece = cut(g, h, source, part)
        pltpu.make_async_remote_copy(
            piece, piece, unit_send.at[g, h, 0, part, 0], unit_recv.at[g, h, source, part],
            device_id=(row, col), device_id_type=MESH).wait_recv()

    def shared(g, h, source_chip):
        piece = held.at[g, h, source_chip * 2 + 1 - core]
        pltpu.make_async_remote_copy(
            piece, piece, pair_send.at[g, h, source_chip], pair_recv.at[g, h, source_chip],
            device_id=(row, col), device_id_type=MESH).wait_recv()

    def send_own(g, h):
        for part in range(per * CUTS):
            branches(g, h, at_x, at_z, start, part)
        share(g, h, chip, start)

    def multiply(g, h, p):
        parts = []
        for q in range(cap):
            for kk in range(2):
                o = p * 2 + kk
                which = brow[q * n_cols + o] % per
                part = held[g, h, o, 0]
                for b in range(1, per):
                    part = jnp.where(which == b, held[g, h, o, b], part)
                parts.append(part)
        high, low = split(jnp.concatenate(parts, axis=0))
        dot = functools.partial(jnp.dot, preferred_element_type=jnp.float32)
        product = dot(w_high[p], high) + dot(w_high[p], low) + dot(w_low[p], high)
        return product.reshape(n_rows, per, tile, LANES)

    def place(turn):
        return nearest(turn // size_x, at_z, size_z), nearest(turn % size_x, at_x, size_x)

    def relay(g, h, turn):
        sz, sx = place(turn)
        p = sz * size_x + sx
        for part in range(per * CUTS):
            arrived(g, h, p * 2 + core, part)
            branches(g, h, sx, sz, start, part)
        share(g, h, p, start)

    def consume(g, h, turn):
        sz, sx = place(turn)
        p = sz * size_x + sx
        shared(g, h, p)
        totals[h] += multiply(g, h, p)

    def turns(low, high, *phases):
        @pl.loop(low, high)
        def _(turn):
            for g, h, shift in phases:
                relay(g, h, turn + shift)
            for g, h, shift in phases:
                consume(g, h, turn + shift - 1)

    def clear(h):
        totals[h] = jnp.zeros_like(totals[h])

    def close(g, h):
        consume(g, h, chips - 1)
        y_start(g, h)

    def y_copy(g, h, step):
        target = (row + step) % n_rows
        return pltpu.make_async_remote_copy(
            totals.at[h, target], partner.at[g, h, row], y_send.at[g, h, step - 1], y_recv.at[g, h, step - 1],
            device_id=(target, col), device_id_type=MESH)

    def y_start(g, h):
        for step in range(1, n_rows):
            y_copy(g, h, step).start()

    def y_drain(g, h):
        for step in range(1, n_rows):
            y_copy(g, h, step).wait_send()

    def y_sum(g, h):
        total = totals[h, row]
        for step in range(1, n_rows):
            origin = (row + n_rows - step) % n_rows
            pltpu.make_async_remote_copy(
                totals.at[h, row], partner.at[g, h, origin], y_send.at[g, h, step - 1], y_recv.at[g, h, step - 1],
                device_id=(row, col), device_id_type=MESH).wait_recv()
            total = total + partner[g, h, origin]
        return total

    def stats_begin(i, rows):
        filler = jnp.zeros((STAT_ROWS - len(rows), LANES), jnp.float32)
        stat_col[i, col] = jnp.concatenate(list(rows) + [filler], axis=0)

        @pl.loop(1, n_cols)
        def _(step):
            pltpu.make_async_remote_copy(
                stat_col.at[i, col], stat_col.at[i, col], col_send.at[i], col_recv.at[i],
                device_id=(row, (col + step) % n_cols), device_id_type=MESH).start()

    def stats_turn(i):
        many = stat_col.at[i, pl.ds(0, n_cols - 1)]
        pltpu.make_async_copy(many, many, col_recv.at[i]).wait()
        stat_row[i, row] = jnp.sum(stat_col[i], axis=0)

        @pl.loop(1, n_rows)
        def _(step):
            pltpu.make_async_remote_copy(
                stat_row.at[i, row], stat_row.at[i, row], row_send.at[i], row_recv.at[i],
                device_id=((row + step) % n_rows, col), device_id_type=MESH).start()

    def stats_end(i):
        many = stat_row.at[i, pl.ds(0, n_rows - 1)]
        pltpu.make_async_copy(many, many, row_recv.at[i]).wait()
        return jnp.sum(stat_row[i], axis=0)

    def stats_drain(i):
        many = stat_col.at[i, pl.ds(0, n_cols - 1)]
        pltpu.make_async_copy(many, many, col_send.at[i]).wait()
        many = stat_row.at[i, pl.ds(0, n_rows - 1)]
        pltpu.make_async_copy(many, many, row_send.at[i]).wait()

    def over_rows(value):
        return jnp.sum(value.reshape(per * tile, LANES), axis=0, keepdims=True)

    for copy in own[:-1]:
        copy.wait()
    send_own(0, 0)
    send_own(0, 1)
    squares = []
    for h in range(halves):
        mine = held[0, h, col]
        squares.append(over_rows(mine * mine))
    stats_begin(0, squares)
    for b in range(per):
        diag[b] = jnp.broadcast_to(diag_ref[pl.ds(b, 1), :], (tile, LANES)).T
    own[-1].wait()

    @pl.loop(0, chips)
    def _(p):
        for q in range(cap):
            for kk in range(2):
                local = p * 2 + kk
                slot = q * n_cols + local
                piece = bcol[slot] // per
                target = piece // n_cols * per + bcol[slot] % per
                target = jnp.where(slot < counts[0], target, -1)
                high, low = split(blocks[slot].T)
                at = pl.ds((q * 2 + kk) * tile, tile)
                for j in range(n_local):
                    keep = jnp.where(target == j, 1.0, 0.0).astype(jnp.bfloat16)
                    w_high[p, pl.ds(j * tile, tile), at] = high * keep
                    w_low[p, pl.ds(j * tile, tile), at] = low * keep

    half = chips // 2 + 1
    rest = min(chips, chips - half + 1)
    late = max(rest, chips - 1)
    clear(0)
    clear(1)
    turns(1, half, (0, 0, 0))
    turns(half, chips, (0, 0, 0), (0, 1, 1 - half))
    close(0, 0)
    stats_turn(0)
    turns(rest, late, (0, 1, 0))
    total_squares = stats_end(0)
    magnitude = [jnp.sqrt(total_squares[k:k + 1] / total_rows + 1e-06) for k in range(2)]
    image_rows = []

    def make_image(h):
        mine = held[0, h, col]
        image = (diag[...] * mine + y_sum(0, h)) / magnitude[h]
        held[1, h, col] = image
        send_own(1, h)
        image_rows.append(over_rows(image * image))
        image_rows.append(over_rows(image * (mine / magnitude[h])))

    make_image(0)
    y_drain(0, 0)
    clear(0)
    turns(late, chips, (0, 1, 0))
    close(0, 1)
    early = min(3, half)
    turns(1, early, (1, 0, 0))
    make_image(1)
    stats_begin(1, image_rows)
    y_drain(0, 1)
    clear(1)
    turns(early, half, (1, 0, 0))
    turns(half, chips, (1, 0, 0), (1, 1, 1 - half))
    close(1, 0)
    stats_turn(1)
    turns(rest, late, (1, 1, 0))
    stats = stats_end(1)
    projection, norm_new = [], []
    for k in range(2):
        image_squares, cross = stats[2 * k:2 * k + 1], stats[2 * k + 1:2 * k + 2]
        basis_squares = total_squares[k:k + 1] / (magnitude[k] * magnitude[k])
        part = cross / total_rows
        power = (image_squares - 2.0 * part * cross + part * part * basis_squares) / total_rows
        projection.append(part)
        norm_new.append(jnp.sqrt(jnp.maximum(power, 0.0) + 1e-06))
        at = pl.ds(k * LANES, LANES)
        image = held[1, k, col].reshape(per * tile, LANES)
        basis = held[0, k, col].reshape(per * tile, LANES) / magnitude[k]
        next_ref[:, at] = (image - part * basis) / norm_new[k]
        column_ref[pl.ds(0, 1), at] = part
        column_ref[pl.ds(1, 1), at] = norm_new[k]
    finish(1, 0, held, diag, projection, norm_new, y_sum, second_ref, col)
    turns(late, chips, (1, 1, 0))
    close(1, 1)
    finish(1, 1, held, diag, projection, norm_new, y_sum, second_ref, col)

    for g in range(2):
        stats_drain(g)
        for h in range(2):
            if g == 1:
                y_drain(g, h)

            @pl.loop(0, chips)
            def _(p):
                for part in range(per * CUTS):
                    branches(g, h, p % size_x, p // size_x, drain, part)
                share(g, h, p, drain)


def finish(g, h, held, diag, projection, norm_new, y_sum, second_ref, col):
    image = held[g, h, col]
    result = (diag[...] * image + y_sum(g, h) - projection[h] * image) / norm_new[h]
    second_ref[:, pl.ds(h * LANES, LANES)] = result.reshape(second_ref.shape[0], LANES)


def per_device(blocks, block_row, block_col, counts, diagonal, vector):
    n_rows, n_cols = lax.axis_size("row"), lax.axis_size("col")
    slots, tile, _ = blocks.shape
    mine, rhs = vector.shape
    per, halves = mine // tile, rhs // LANES
    cap, chips, n_local = slots // n_cols, n_cols // 2, n_rows * per
    smem = pl.BlockSpec(memory_space=pltpu.SMEM)
    vmem = pl.BlockSpec(memory_space=pltpu.VMEM)
    anywhere = pl.BlockSpec(memory_space=pl.ANY)
    f32, dma = jnp.float32, pltpu.SemaphoreType.DMA
    weight = pltpu.VMEM((chips, n_local * tile, 2 * cap * tile), jnp.bfloat16)
    return pl.pallas_call(
        functools.partial(kernel, n_rows, n_cols, mine * n_rows * n_cols),
        out_shape=(
            jax.ShapeDtypeStruct((mine, rhs), f32),
            jax.ShapeDtypeStruct((mine, rhs), f32),
            jax.ShapeDtypeStruct((2, rhs), f32),
        ),
        in_specs=[smem, smem, smem, anywhere, vmem, anywhere],
        out_specs=(vmem, vmem, vmem),
        scratch_shapes=[
            pltpu.VMEM((slots, tile, tile), f32),
            pltpu.VMEM((2, halves, n_cols, per, tile, LANES), f32),
            weight,
            weight,
            pltpu.VMEM((halves, n_rows, per, tile, LANES), f32),
            pltpu.VMEM((2, halves, n_rows, per, tile, LANES), f32),
            pltpu.VMEM((per, tile, LANES), f32),
            pltpu.VMEM((2, n_cols, STAT_ROWS, LANES), f32),
            pltpu.VMEM((2, n_rows, STAT_ROWS, LANES), f32),
            dma((halves * per + 1,)),
            dma((2, halves, chips, per * CUTS, 4)),
            dma((2, halves, n_cols, per * CUTS)),
            dma((2, halves, chips)),
            dma((2, halves, chips)),
            dma((2, halves, n_rows)),
            dma((2, halves, n_rows)),
            dma((2,)), dma((2,)), dma((2,)), dma((2,)),
        ],
        compiler_params=pltpu.CompilerParams(
            collective_id=0, has_side_effects=True, vmem_limit_bytes=60 * 1024 * 1024),
    )(block_row, block_col, counts, blocks, diagonal.reshape(per, tile), vector)


def solution(mesh):
    spec = P(("row", "col"))
    return jax.shard_map(
        per_device,
        mesh=mesh,
        in_specs=(P(("row", "col"), None, None), spec, spec, spec, spec, P(("row", "col"), None)),
        out_specs=(P(("row", "col"), None), P(("row", "col"), None), P()),
        check_vma=False,
    )
```
